128 devices in a mesh: section: 32 (over z, y, x_lo), expert: 2 (over core), shard: 2 (over x_hi).
Axes of the slice: x: 4 (x_hi: 2, x_lo: 2; x = x_hi * 2 + x_lo), y: 4, z: 4, core: 2. Of those that a mesh axis runs over, the one named last changes fastest.
Arguments:
- routes: int32 [32, 4, 64, 2], P('section', None, 'expert'), may hold values from 0 to 7, as said below
- route_probs: float32 [32, 4, 64, 2], P('section', None, 'expert'), may hold values from 0.2 to 1
- example_ids: int32 [4, 2, 32], P(None, 'expert'), may hold values from 0 to 1, never falling along the last dimension, each value on 1 to 24 neighbouring positions
- top_cotangent: bfloat16 [4, 64, 6144], P(None, 'expert', 'shard'), may hold values from -6 to 6
- branch_cotangent: bfloat16 [32, 4, 64, 6144], P('section', None, 'expert', 'shard'), may hold values from -4 to 4
- hidden_acts: bfloat16 [32, 2, 4, 32, 16384], P('section', 'expert', None, None, 'shard'), may hold values from -6 to 6
- basis_hidden: bfloat16 [32, 2, 16384, 256], P('section', 'expert', 'shard'), may hold values from -0.046875 to 0.046875
- basis_model: bfloat16 [32, 2, 6144, 1024], P('section', 'expert', 'shard'), may hold values from -0.078125 to 0.078125
Outputs:
- eigen_correction: float32 [32, 2, 256, 1024], P('section', 'expert', None, 'shard')
The draws below stay inside these ranges and needn't reach their ends.
Inputs may be any that keep to these rules, and one draw needn't show every extreme that they name: `routes`: each token names 2 different experts of the 8. Within the 32 tokens of one owner in one micro-batch no expert is named more than 16 times, and exactly one expert is named 16 times. In one micro-batch of every layer that expert is the same for every owner and is below 2. `example_ids`: Non-decreasing along each owner's 32 tokens of a micro-batch; each example has 1 to 24 tokens.
All inputs are finite; a program needn't handle non-finite values.
Results may differ from the reference program's by a relative error of at most 0.0047.
Values may be sent and summed in bfloat16 or wider, within the bound.
No kernel may reach another device: no remote copies, remote signals or barrier semaphores. Data moves between devices by JAX's collectives and lax.ppermute only.
A program may use at most 128 MiB of HBM per device.

```python
import math
import jax
import jax.numpy as jnp
import numpy as np
from jax import lax

D = 6144
FF = 16384
ROUTED = 8
TOP = 2
MB = 4
TOK_MB = 32
SEQS = 2
KI = 256
KJ = 1024
SECTIONS = 32
EXPERTS = 2
OWNERS = 2
TOKENS = 64
CAP = 16
SLOTS = 32
LONGEST = 24
N_EXPERT = 2


def route_block(block_key, hot_expert):
    key_list = jax.random.split(block_key, 4)
    token_rank = jnp.arange(TOK_MB, dtype=jnp.int32)
    order_score = jax.random.randint(key_list[0], (TOK_MB,), 0, 1 << 20) * TOK_MB + token_rank
    token_order = jnp.argsort(order_score).astype(jnp.int32)
    others = ROUTED - 1
    name_count = TOK_MB + CAP
    spread = name_count // (3 * others)
    cut_points = jnp.arange(1, others, dtype=jnp.int32) * name_count // others
    cut_points = cut_points + jax.random.randint(key_list[1], (others - 1,), -spread, spread + 1)
    position = jnp.arange(name_count, dtype=jnp.int32)
    run_index = jnp.sum((position[:, None] >= cut_points[None, :]).astype(jnp.int32), axis=1)
    shuffle_score = jax.random.randint(key_list[2], (others,), 0, 1 << 20) * others + jnp.arange(others, dtype=jnp.int32)
    run_owner = jnp.argsort(shuffle_score).astype(jnp.int32)
    picked = run_owner[run_index]
    named_other = jnp.where(picked >= hot_expert, picked + 1, picked)
    in_hot = token_rank < CAP
    first_name = jnp.where(in_hot, hot_expert, named_other[:TOK_MB])
    second_at = jnp.where(in_hot, token_rank, TOK_MB + token_rank - CAP)
    second_name = named_other[second_at]
    flipped = jax.random.randint(key_list[3], (TOK_MB,), 0, 2) == 1
    paired = jnp.stack([jnp.where(flipped, second_name, first_name), jnp.where(flipped, first_name, second_name)], axis=1)
    inverse = jnp.argsort(token_order).astype(jnp.int32)
    return paired[inverse]


def draw_routes(key, part):
    block_total = SECTIONS * MB * OWNERS
    key_list = jax.random.split(jax.random.fold_in(key, 11), 4)
    free_hot = jax.random.randint(key_list[0], (SECTIONS, MB, OWNERS), 0, ROUTED)
    theme_expert = jax.random.randint(key_list[1], (SECTIONS, 1, 1), 0, EXPERTS)
    forced_batch = jax.random.randint(key_list[2], (SECTIONS, 1, 1), 0, MB)
    batch_rank = jnp.arange(MB, dtype=jnp.int32)[None, :, None]
    hot_expert = jnp.where(batch_rank == forced_batch, theme_expert, free_hot).reshape(block_total)
    block_keys = jax.random.split(key_list[3], block_total)
    paired = jax.vmap(route_block)(block_keys, hot_expert)
    return paired.reshape(SECTIONS, MB, OWNERS * TOK_MB, TOP).astype(jnp.int32)


def block_levels(rng, dims, pieces, low, high):
    def one(axis_at, parts):
        steps = jax.random.uniform(jax.random.fold_in(jax.random.fold_in(rng, 6), axis_at), (parts,), jnp.float32, low / len(pieces), high / len(pieces))
        return jnp.repeat(jnp.exp(steps), dims[axis_at] // parts).reshape((-1,) + (1,) * (len(dims) - axis_at - 1))

    level = one(*pieces[0])
    for cut in pieces[1:]:
        level = level * one(*cut)
    return level


def length_profile(count, total, reach, lean):
    portions = [(1 << 20) // math.isqrt(grade ** lean) + 1 for grade in range(2, count + 1)]
    surplus, counts = total - reach - (count - 1), [1] * (count - 1)
    while surplus > 0:
        candidates = [i for i in range(count - 1) if counts[i] < reach]
        mass, budget = sum([portions[i] for i in candidates]), surplus
        for i in candidates:
            more = min(reach - counts[i], max(1, budget * portions[i] // mass), surplus)
            counts[i] = counts[i] + more
            surplus = surplus - more
    return np.array([reach] + counts)


def ragged_sizes(key, number_of, total, bound, lean):
    if number_of == 2:
        one = jax.random.randint(key, (), max(1, total - bound), min(bound, total - 1) + 1)
        return jnp.stack([one, total - one])
    sizes = jnp.asarray(length_profile(number_of, total, bound, lean), jnp.int32)
    couples = (number_of - 1) // 2
    source_of, receiver = sizes[1:1 + 2 * couples:2], sizes[2:2 + 2 * couples:2]
    slack = jnp.minimum(source_of - 1, bound - receiver)
    shifted = jax.random.randint(jax.random.fold_in(key, 1), (couples,), 0, 1 << 20) % (slack + 1)
    sizes = sizes.at[1:1 + 2 * couples:2].set(source_of - shifted).at[2:2 + 2 * couples:2].set(receiver + shifted)
    return sizes[jax.random.permutation(jax.random.fold_in(key, 2), number_of)]


def gaussian(stream_key, dims, deviation, most, shards=(), held_as=jnp.bfloat16):
    result = deviation * jax.random.normal(stream_key, dims, jnp.float32)
    if shards:
        result = result * block_levels(stream_key, dims, shards, -0.22, 0.18)
    return jnp.clip(result, -most, most).astype(held_as)


def setup_inputs(seed: int = 0) -> dict:
    splits = jax.random.split(jax.random.key(seed), 9)
    routes = draw_routes(jax.random.fold_in(splits[8], 71), 0)
    route_probs = jnp.clip(0.2 + 0.8 * jax.random.uniform(splits[1], (SECTIONS, MB, TOKENS, TOP), jnp.float32) ** block_levels(splits[1], (SECTIONS, MB, TOKENS, TOP), ((0, 32), (2, 2)), -0.2, 0.2), 0.2, 1.0)
    example_ids = jax.vmap(lambda own: jnp.searchsorted(jnp.cumsum(ragged_sizes(own, SEQS, TOK_MB, LONGEST, 1)), jnp.arange(TOK_MB), side="right"))(jax.random.split(splits[2], MB * OWNERS)).reshape((MB, OWNERS, TOK_MB)).astype(jnp.int32)
    top_cotangent = gaussian(splits[3], (MB, TOKENS, D), 1.0, 6.0, ((1, 2), (2, 2)))
    branch_cotangent = gaussian(splits[4], (SECTIONS, MB, TOKENS, D), 0.5, 4.0, ((0, 32), (2, 2), (3, 2)))
    hidden_acts = gaussian(splits[5], (SECTIONS, EXPERTS, MB, SLOTS, FF), 1.0, 6.0, ((0, 32), (1, 2), (4, 2)))
    basis_hidden = gaussian(splits[6], (SECTIONS, EXPERTS, FF, KI), FF ** -0.5, 0.046875, ((0, 32), (1, 2), (2, 2)))
    basis_model = gaussian(splits[7], (SECTIONS, EXPERTS, D, KJ), D ** -0.5, 0.078125, ((0, 32), (1, 2), (2, 2)))
    return dict(routes=routes, route_probs=route_probs, example_ids=example_ids, top_cotangent=top_cotangent, branch_cotangent=branch_cotangent, hidden_acts=hidden_acts, basis_hidden=basis_hidden, basis_model=basis_model)


def dispatch_tables(route_rows, prob_rows, example_rows, experts, capacity):
    expert_hit = (route_rows[:, :, :, None] == jnp.arange(experts, dtype=jnp.int32)).astype(jnp.int32)
    expert_count = jnp.sum(expert_hit, axis=2)
    slot_rank = jnp.cumsum(expert_count, axis=1) - expert_count
    expert_prob = jnp.sum(expert_hit.astype(jnp.float32) * prob_rows[:, :, :, None], axis=2)
    slot_match = (slot_rank[:, :, :, None] == jnp.arange(capacity, dtype=jnp.int32)) & (expert_count[:, :, :, None] > 0)
    dispatch_weight = jnp.where(slot_match, expert_prob[:, :, :, None], jnp.float32(0.0))
    slot_example = jnp.sum(jnp.where(slot_match, example_rows[:, :, None, None] + 1, 0), axis=1) - 1
    return dispatch_weight, slot_example.astype(jnp.int32)


def example_squares(rotated_hidden, rotated_model, slot_example, examples):
    member = slot_example[:, None, :] == jnp.arange(examples, dtype=jnp.int32)[None, :, None]
    masked = jnp.where(member[:, :, :, None], rotated_hidden[:, None, :, :].astype(jnp.float32), jnp.float32(0.0))
    example_grad = jnp.einsum("osci,ocj->osij", masked, rotated_model.astype(jnp.float32))
    return jnp.sum(example_grad * example_grad, axis=(0, 1))


def reference(routes, route_probs, example_ids, top_cotangent, branch_cotangent, hidden_acts, basis_hidden, basis_model):
    owners = N_EXPERT
    branch_wide = branch_cotangent.astype(jnp.float32)
    suffix_sum = jnp.cumsum(branch_wide[::-1], axis=0)[::-1]
    later_all = jnp.concatenate([suffix_sum[1:], jnp.zeros_like(suffix_sum[:1])], axis=0)
    layer_list = []
    for layer_now in range(SECTIONS):
        cotangent = (top_cotangent.astype(jnp.float32) + later_all[layer_now]).reshape(MB * owners, TOK_MB, D)
        dispatch_weight, slot_example = dispatch_tables(
            routes[layer_now].reshape(MB * owners, TOK_MB, TOP),
            route_probs[layer_now].reshape(MB * owners, TOK_MB, TOP),
            example_ids.reshape(MB * owners, TOK_MB), EXPERTS, CAP)
        send_rows = jnp.einsum("ntec,ntd->necd", dispatch_weight, cotangent, precision=lax.Precision.HIGHEST).astype(jnp.bfloat16)
        send_rows = send_rows.reshape(MB, owners, EXPERTS, CAP, D)
        slot_example = slot_example.reshape(MB, owners, EXPERTS, CAP)
        expert_list = []
        for expert_now in range(EXPERTS):
            model_rows = send_rows[:, :, expert_now].astype(jnp.float32)
            rotated_model = jnp.einsum("mocd,dk->mock", model_rows, basis_model[layer_now, expert_now].astype(jnp.float32)).astype(jnp.bfloat16)
            rotated_hidden = jnp.einsum("msf,fk->msk", hidden_acts[layer_now, expert_now].astype(jnp.float32), basis_hidden[layer_now, expert_now].astype(jnp.float32)).astype(jnp.bfloat16)
            rotated_hidden = rotated_hidden.reshape(MB, owners, CAP, KI)
            square_sum = jnp.zeros((KI, KJ), jnp.float32)
            for micro_batch in range(MB):
                square_sum = square_sum + example_squares(rotated_hidden[micro_batch], rotated_model[micro_batch], slot_example[micro_batch, :, expert_now], SEQS)
            expert_list.append(square_sum / (MB * owners * SEQS))
        layer_list.append(jnp.stack(expert_list))
    return jnp.stack(layer_list)
```

```python
import functools

import jax
import jax.numpy as jnp
from jax import lax
from jax.experimental import pallas as pl
from jax.experimental.pallas import tpu as pltpu
from jax.sharding import PartitionSpec as P

SEQS = 2
TAG = 128


def scan_kernel(x_ref, o_ref):
    count = x_ref.shape[0]
    state = jnp.zeros(x_ref.shape[1:], jnp.float32)
    for place in range(count - 1, -1, -1):
        o_ref[place] = state.astype(jnp.bfloat16)
        if place:
            state = state + x_ref[place].astype(jnp.float32)


def dispatch_kernel(
    later_ref, top_ref, routes_ref, probs_ref, ids_ref, kept_ref, sent_ref, *, capacity
):
    batches, tokens, width = top_ref.shape
    rows, part = later_ref.shape[1:]
    halves = width // part
    blocks = tokens // rows
    mine = lax.axis_index("expert")
    before = (
        lax.broadcasted_iota(jnp.int32, (tokens, tokens), 0)
        < lax.broadcasted_iota(jnp.int32, (tokens, tokens), 1)
    ).astype(jnp.bfloat16)
    eye = lax.broadcasted_iota(jnp.int32, (tokens, tokens), 0) == lax.broadcasted_iota(
        jnp.int32, (tokens, tokens), 1
    )
    slot = lax.broadcasted_iota(jnp.int32, (capacity, tokens), 0).astype(jnp.float32)
    for m in range(batches):
        names = routes_ref[m]
        weights = probs_ref[m]
        examples = ids_ref[m : m + 1].astype(jnp.float32) + 1.0
        for target, out_ref in ((mine, kept_ref), (1 - mine, sent_ref)):
            hit2 = names == target
            hit = jnp.sum(hit2.astype(jnp.float32), axis=0, keepdims=True)
            weight = jnp.sum(jnp.where(hit2, weights, 0.0), axis=0, keepdims=True)
            rank = jnp.dot(
                jnp.broadcast_to(hit, (8, tokens)).astype(jnp.bfloat16),
                before,
                preferred_element_type=jnp.float32,
            )[:1]
            chosen = (jnp.broadcast_to(rank, slot.shape) == slot) & (
                jnp.broadcast_to(hit, slot.shape) > 0.0
            )
            pick = chosen.astype(jnp.bfloat16)
            tag = (
                jnp.sum(
                    jnp.where(chosen, jnp.broadcast_to(examples, slot.shape), 0.0),
                    axis=1,
                    keepdims=True,
                )
                - 1.0
            )
            scale = jnp.sum(
                jnp.where(eye, jnp.broadcast_to(weight, eye.shape), 0.0),
                axis=1,
                keepdims=True,
            )
            at = pl.ds(m * capacity, capacity)
            for h in range(halves):
                cols = pl.ds(h * part, part)
                later = jnp.concatenate(
                    [
                        later_ref[(m * blocks + b) * halves + h].astype(jnp.float32)
                        for b in range(blocks)
                    ],
                    axis=0,
                )
                value = top_ref[m, :, cols].astype(jnp.float32) + later
                value = (value * scale).astype(jnp.bfloat16)
                out_ref[at, cols] = jnp.dot(
                    pick, value, preferred_element_type=jnp.float32
                ).astype(jnp.bfloat16)
            out_ref[at, pl.ds(width, TAG)] = jnp.broadcast_to(
                tag, (capacity, TAG)
            ).astype(jnp.bfloat16)


def rotate_kernel(kept_ref, got_ref, basis_ref, out_ref, *, mine):
    width, cols = basis_ref.shape
    half = cols // 2
    place = lax.axis_index("shard")
    start = pl.multiple_of((place if mine else 1 - place) * half, half)
    rows = jnp.concatenate([kept_ref[:, :width], got_ref[:, :width]], axis=0)
    out_ref[...] = jnp.dot(
        rows, basis_ref[:, pl.ds(start, half)], preferred_element_type=jnp.float32
    ).astype(out_ref.dtype)


def square_kernel(
    kept_ref, got_ref, model_ref, model_far_ref, hidden_ref, hidden_far_ref, out_ref, *, capacity, owners
):
    total = model_ref.shape[0]
    width = kept_ref.shape[1] - TAG
    batches = total // (owners * capacity)
    mine = lax.axis_index("expert")
    acc = None
    for side, rows_ref in enumerate((kept_ref, got_ref)):
        owner = mine if side == 0 else 1 - mine
        for m in range(batches):
            at = pl.ds(side * batches * capacity + m * capacity, capacity)
            model = (model_ref[at, :] + model_far_ref[at, :].astype(jnp.float32)).astype(
                jnp.bfloat16
            )
            slots = pl.ds(
                pl.multiple_of(m * owners * capacity + owner * capacity, capacity), capacity
            )
            hidden = hidden_ref[slots, :] + hidden_far_ref[slots, :].astype(jnp.float32)
            tag = rows_ref[pl.ds(m * capacity, capacity), pl.ds(width, TAG)].astype(jnp.float32)
            tag = jnp.concatenate([tag] * (hidden.shape[1] // TAG), axis=1)
            for q in range(SEQS):
                masked = jnp.where(tag == float(q), hidden, 0.0).astype(jnp.bfloat16)
                grad = lax.dot_general(
                    masked, model, (((0,), (0,)), ((), ())), preferred_element_type=jnp.float32
                )
                acc = grad * grad if acc is None else acc + grad * grad
    out_ref[...] = acc * (1.0 / (batches * owners * SEQS))


VMEM = pl.BlockSpec(memory_space=pltpu.VMEM)


def call(body, shapes, ins):
    single = not isinstance(shapes, (list, tuple))
    return pl.pallas_call(
        body,
        out_shape=shapes,
        in_specs=[VMEM] * ins,
        out_specs=VMEM if single else [VMEM] * len(shapes),
    )


def on_device(
    routes,
    route_probs,
    example_ids,
    top_cotangent,
    branch_cotangent,
    hidden_acts,
    basis_hidden,
    basis_model,
):
    experts = lax.axis_size("expert")
    shards = lax.axis_size("shard")
    sections = lax.axis_size("section")
    batches, tokens, width = top_cotangent.shape
    slots = hidden_acts.shape[3]
    capacity = slots // experts
    cols = basis_model.shape[3]
    kept_cols = cols // shards
    rank = basis_hidden.shape[3]
    rows = batches * experts * capacity
    block = 8
    groups = batches * tokens // block
    halves = sections // groups
    part = width // halves

    hidden = jnp.dot(
        hidden_acts[0, 0].reshape(rows, -1),
        basis_hidden[0, 0],
        preferred_element_type=jnp.float32,
    )
    pieces = (
        branch_cotangent[0]
        .reshape(groups, block, halves, part)
        .transpose(0, 2, 1, 3)
        .reshape(sections, block, part)
    )
    layers = lax.all_to_all(pieces, "section", 0, 0, tiled=True)
    layers = call(scan_kernel, jax.ShapeDtypeStruct(layers.shape, jnp.bfloat16), 1)(layers)
    later = lax.all_to_all(layers, "section", 0, 0, tiled=True)
    row_shape = jax.ShapeDtypeStruct((batches * capacity, width + TAG), jnp.bfloat16)
    kept, sent = call(
        functools.partial(dispatch_kernel, capacity=capacity), [row_shape, row_shape], 5
    )(
        later,
        top_cotangent,
        routes[0].transpose(0, 2, 1),
        route_probs[0].transpose(0, 2, 1),
        example_ids[:, 0],
    )
    swap = [(0, 1), (1, 0)]
    got = lax.ppermute(sent, "expert", swap)
    model_send = call(
        functools.partial(rotate_kernel, mine=False),
        jax.ShapeDtypeStruct((rows, kept_cols), jnp.bfloat16),
        3,
    )(kept, got, basis_model[0, 0])
    far = lax.ppermute(model_send, "shard", swap)
    hidden_far = lax.ppermute(hidden.astype(jnp.bfloat16), "shard", swap)
    model = call(
        functools.partial(rotate_kernel, mine=True),
        jax.ShapeDtypeStruct((rows, kept_cols), jnp.float32),
        3,
    )(kept, got, basis_model[0, 0])
    out = call(
        functools.partial(square_kernel, capacity=capacity, owners=experts),
        jax.ShapeDtypeStruct((rank, kept_cols), jnp.float32),
        6,
    )(kept, got, model, far, hidden, hidden_far)
    return out[None, None]


def solution(mesh):
    return jax.shard_map(
        on_device,
        mesh=mesh,
        in_specs=(
            P("section", None, "expert", None),
            P("section", None, "expert", None),
            P(None, "expert", None),
            P(None, "expert", "shard"),
            P("section", None, "expert", "shard"),
            P("section", "expert", None, None, "shard"),
            P("section", "expert", "shard", None),
            P("section", "expert", "shard", None),
        ),
        out_specs=P("section", "expert", None, "shard"),
        check_vma=False,
    )
```

```python
import functools

import jax
import jax.numpy as jnp
from jax import lax
from jax.experimental import pallas as pl
from jax.experimental.pallas import tpu as pltpu
from jax.sharding import PartitionSpec as P

SEQS = 2
LANES = 128


def scan_kernel(x_ref, o_ref):
    count = x_ref.shape[0]
    state = jnp.zeros(x_ref.shape[1:], jnp.float32)
    for place in range(count - 1, -1, -1):
        o_ref[place] = state.astype(jnp.bfloat16)
        if place:
            state = state + x_ref[place].astype(jnp.float32)


def prepare_kernel(
    routes_ref,
    probs_ref,
    ids_ref,
    top_ref,
    pick_ref,
    scale_ref,
    tag_ref,
    tag_sent_ref,
    held_ref,
    sem,
    *,
    capacity
):
    batches, _, tokens = routes_ref.shape
    mine = lax.axis_index("expert")
    load = pltpu.make_async_copy(top_ref, held_ref, sem)
    load.start()
    before = (
        lax.broadcasted_iota(jnp.int32, (tokens, tokens), 0)
        < lax.broadcasted_iota(jnp.int32, (tokens, tokens), 1)
    ).astype(jnp.bfloat16)
    eye = lax.broadcasted_iota(jnp.int32, (tokens, tokens), 0) == lax.broadcasted_iota(
        jnp.int32, (tokens, tokens), 1
    )
    slot = lax.broadcasted_iota(jnp.int32, (capacity, tokens), 0).astype(jnp.float32)
    for m in range(batches):
        names = routes_ref[m]
        weights = probs_ref[m]
        examples = ids_ref[m : m + 1].astype(jnp.float32) + 1.0
        for side in range(2):
            hit2 = names == (1 - mine if side else mine)
            hit = jnp.sum(hit2.astype(jnp.float32), axis=0, keepdims=True)
            weight = jnp.sum(jnp.where(hit2, weights, 0.0), axis=0, keepdims=True)
            rank = jnp.dot(
                jnp.broadcast_to(hit, (8, tokens)).astype(jnp.bfloat16),
                before,
                preferred_element_type=jnp.float32,
            )[:1]
            chosen = (jnp.broadcast_to(rank, slot.shape) == slot) & (
                jnp.broadcast_to(hit, slot.shape) > 0.0
            )
            pick = chosen.astype(jnp.float32)
            blank = jnp.zeros(pick.shape, jnp.float32)
            row = jnp.concatenate([pick if n == m else blank for n in range(batches)], axis=1)
            pick_ref[side, pl.ds(m * capacity, capacity), :] = row.astype(jnp.bfloat16)
            tag = (
                jnp.sum(
                    jnp.where(chosen, jnp.broadcast_to(examples, slot.shape), 0.0),
                    axis=1,
                    keepdims=True,
                )
                - 1.0
            )
            (tag_sent_ref if side else tag_ref)[pl.ds(m * capacity, capacity), :] = (
                jnp.broadcast_to(tag, (capacity, LANES)).astype(jnp.bfloat16)
            )
            scale = jnp.sum(
                jnp.where(eye, jnp.broadcast_to(weight, eye.shape), 0.0),
                axis=1,
                keepdims=True,
            )
            scale_ref[side, pl.ds(m * tokens, tokens), :] = jnp.broadcast_to(
                scale, (tokens, LANES)
            )
    load.wait()


def hidden_kernel(acts_ref, basis_ref, out_ref, acts_held, basis_held, sems):
    count = sems.shape[1]
    depth = acts_ref.shape[1] // count
    copies = []
    for k in range(count):
        at = pl.ds(k * depth, depth)
        pair = (
            pltpu.make_async_copy(acts_ref.at[:, at], acts_held.at[:, at], sems.at[0, k]),
            pltpu.make_async_copy(basis_ref.at[at, :], basis_held.at[at, :], sems.at[1, k]),
        )
        for copy in pair:
            copy.start()
        copies.append(pair)
    total = None
    for k in range(count):
        at = pl.ds(k * depth, depth)
        for copy in copies[k]:
            copy.wait()
        part = jnp.dot(acts_held[:, at], basis_held[at, :], preferred_element_type=jnp.float32)
        total = part if total is None else total + part
    out_ref[...] = total


def mask_kernel(hidden_ref, far_ref, tag_ref, tag_far_ref, out_ref, *, capacity, owners):
    batches = hidden_ref.shape[0] // (owners * capacity)
    mine = lax.axis_index("expert")
    for side in range(2):
        owner = 1 - mine if side else mine
        for m in range(batches):
            slots = pl.ds(
                pl.multiple_of(m * owners * capacity + owner * capacity, capacity), capacity
            )
            at = pl.ds(m * capacity, capacity)
            hidden = hidden_ref[slots, :] + far_ref[slots, :].astype(jnp.float32)
            tag = (tag_far_ref if side else tag_ref)[at, :].astype(jnp.float32)
            tag = jnp.concatenate([tag] * (hidden.shape[1] // LANES), axis=1)
            for q in range(SEQS):
                out_ref[side, q, at, :] = jnp.where(tag == float(q), hidden, 0.0).astype(
                    jnp.bfloat16
                )


def dispatch(later_ref, top_ref, pick_ref, scale_ref, side, store):
    batches, tokens, width = top_ref.shape
    rows, part = later_ref.shape[1:]
    halves = width // part
    blocks = tokens // rows
    step = 2 * LANES
    for h in range(halves):
        for c in range(0, part, step):
            values = []
            for m in range(batches):
                for b in range(blocks):
                    later = later_ref[(m * blocks + b) * halves + h, :, pl.ds(c, step)]
                    top = top_ref[m, pl.ds(b * rows, rows), pl.ds(h * part + c, step)]
                    scale = scale_ref[side, pl.ds(m * tokens + b * rows, rows), :]
                    scale = jnp.concatenate([scale] * (step // LANES), axis=1)
                    values.append((top.astype(jnp.float32) + later.astype(jnp.float32)) * scale)
            value = jnp.concatenate(values, axis=0).astype(jnp.bfloat16)
            store(
                h * part + c,
                step,
                jnp.dot(pick_ref[side], value, preferred_element_type=jnp.float32).astype(
                    jnp.bfloat16
                ),
            )


def sent_kernel(later_ref, top_ref, pick_ref, scale_ref, out_ref):
    def store(at, size, value):
        out_ref[:, pl.ds(at, size)] = value

    dispatch(later_ref, top_ref, pick_ref, scale_ref, 1, store)


def stream_half(source, target, sems, mine):
    count = sems.shape[0]
    depth = source.shape[0] // count
    half = target.shape[1]
    place = lax.axis_index("shard")
    start = pl.multiple_of((place if mine else 1 - place) * half, half)
    copies = []
    for k in range(count):
        at = pl.ds(k * depth, depth)
        copy = pltpu.make_async_copy(
            source.at[at, pl.ds(start, half)], target.at[at, :], sems.at[k]
        )
        copy.start()
        copies.append(copy)
    return copies


def rotate(blocks, basis_ref, copies=None):
    count = 1 if copies is None else len(copies)
    depth = basis_ref.shape[0] // count
    total = None
    for k in range(count):
        at = pl.ds(k * depth, depth)
        if copies is not None:
            copies[k].wait()
        rows = [ref[:, at] for ref in blocks]
        part = jnp.dot(
            rows[0] if len(rows) == 1 else jnp.concatenate(rows, axis=0),
            basis_ref[at, :],
            preferred_element_type=jnp.float32,
        )
        total = part if total is None else total + part
    return total


def kept_kernel(
    later_ref, top_ref, pick_ref, scale_ref, basis_ref, send_ref, rows_ref, held_ref, sems
):
    copies = stream_half(basis_ref, held_ref, sems, False)

    def store(at, size, value):
        rows_ref[:, pl.ds(at, size)] = value

    dispatch(later_ref, top_ref, pick_ref, scale_ref, 0, store)
    send_ref[...] = rotate([rows_ref], held_ref, copies).astype(send_ref.dtype)


def got_kernel(rows_ref, held_ref, send_ref):
    send_ref[...] = rotate([rows_ref], held_ref).astype(send_ref.dtype)


def keep_kernel(kept_ref, got_ref, basis_ref, out_ref, held_ref, sems):
    copies = stream_half(basis_ref, held_ref, sems, True)
    out_ref[...] = rotate([kept_ref, got_ref], held_ref, copies)


def square_kernel(model_ref, far_ref, hidden_ref, *rest, capacity, side, count):
    out_ref = rest[-1]
    acc = rest[0][...] if len(rest) > 1 else None
    rows = far_ref.shape[0]
    for m in range(rows // capacity):
        at = pl.ds(m * capacity, capacity)
        near = pl.ds(side * rows + m * capacity, capacity)
        model = (model_ref[near, :] + far_ref[at, :].astype(jnp.float32)).astype(jnp.bfloat16)
        for q in range(SEQS):
            grad = lax.dot_general(
                hidden_ref[side, q, at, :],
                model,
                (((0,), (0,)), ((), ())),
                preferred_element_type=jnp.float32,
            )
            acc = grad * grad if acc is None else acc + grad * grad
    if side:
        acc = acc * (1.0 / count)
    out_ref[...] = acc


VMEM = pl.BlockSpec(memory_space=pltpu.VMEM)
HBM = pl.BlockSpec(memory_space=pltpu.HBM)


def call(body, shapes, ins, limit=8 << 20, scratch=()):
    single = not isinstance(shapes, (list, tuple))
    return pl.pallas_call(
        body,
        scratch_shapes=scratch,
        out_shape=shapes,
        in_specs=[VMEM] * ins if isinstance(ins, int) else ins,
        out_specs=VMEM if single else [VMEM] * len(shapes),
        compiler_params=pltpu.CompilerParams(vmem_limit_bytes=limit),
    )


def on_device(
    routes,
    route_probs,
    example_ids,
    top_cotangent,
    branch_cotangent,
    hidden_acts,
    basis_hidden,
    basis_model,
):
    experts = lax.axis_size("expert")
    shards = lax.axis_size("shard")
    sections = lax.axis_size("section")
    batches, tokens, width = top_cotangent.shape
    slots = hidden_acts.shape[3]
    capacity = slots // experts
    cols = basis_model.shape[3]
    kept_cols = cols // shards
    rank = basis_hidden.shape[3]
    rows = batches * experts * capacity
    block = 8
    groups = batches * tokens // block
    halves = sections // groups
    part = width // halves

    swap = [(0, 1), (1, 0)]
    shape = jax.ShapeDtypeStruct
    fixed = functools.partial(pltpu.with_memory_space_constraint, memory_space=pltpu.HBM)
    basis = fixed(basis_model[0, 0])
    acts = hidden_acts[0, 0].reshape(rows, -1)
    hidden = call(
        hidden_kernel,
        shape((rows, rank), jnp.float32),
        [HBM] * 2,
        limit=16 << 20,
        scratch=[
            pltpu.VMEM(acts.shape, jnp.bfloat16),
            pltpu.VMEM(basis_hidden.shape[2:], jnp.bfloat16),
            pltpu.SemaphoreType.DMA((2, 8)),
        ],
    )(fixed(acts), fixed(basis_hidden[0, 0]))
    pieces = (
        branch_cotangent[0]
        .reshape(groups, block, halves, part)
        .transpose(0, 2, 1, 3)
        .reshape(sections, block, part)
    )
    hidden_far = lax.ppermute(hidden.astype(jnp.bfloat16), "shard", swap)
    tag_shape = shape((batches * capacity, LANES), jnp.bfloat16)
    pick, scale, tag, tag_sent, top = call(
        functools.partial(prepare_kernel, capacity=capacity),
        [
            shape((2, batches * capacity, batches * tokens), jnp.bfloat16),
            shape((2, batches * tokens, LANES), jnp.float32),
            tag_shape,
            tag_shape,
            pltpu.VMEM(top_cotangent.shape, jnp.bfloat16),
        ],
        [VMEM] * 3 + [HBM],
        scratch=[pltpu.SemaphoreType.DMA],
    )(
        routes[0].transpose(0, 2, 1),
        route_probs[0].transpose(0, 2, 1),
        example_ids[:, 0],
        fixed(top_cotangent),
    )
    tag_far = lax.ppermute(tag_sent, "expert", swap)
    layers = lax.all_to_all(pieces, "section", 0, 0, tiled=True)
    layers = call(scan_kernel, shape(layers.shape, jnp.bfloat16), 1)(layers)
    layers, hidden, hidden_far, pick, scale, top, tag, tag_far = lax.optimization_barrier(
        (layers, hidden, hidden_far, pick, scale, top, tag, tag_far)
    )
    later = lax.all_to_all(layers, "section", 0, 0, tiled=True)
    masked = call(
        functools.partial(mask_kernel, capacity=capacity, owners=experts),
        shape((2, SEQS, batches * capacity, rank), jnp.bfloat16),
        4,
    )(hidden, hidden_far, tag, tag_far)
    half = (batches * capacity, kept_cols)
    row_shape = shape((batches * capacity, width), jnp.bfloat16)
    near_shape = pltpu.VMEM((width, kept_cols), jnp.bfloat16)
    sent = call(sent_kernel, row_shape, 4)(later, top, pick, scale)
    got = lax.ppermute(sent, "expert", swap)
    send_kept, kept, held = call(
        kept_kernel,
        [shape(half, jnp.bfloat16), row_shape, near_shape],
        [VMEM] * 4 + [HBM],
        scratch=[pltpu.SemaphoreType.DMA((4,))],
    )(later, top, pick, scale, basis)
    far_kept = lax.ppermute(send_kept, "shard", swap)
    send_got = call(got_kernel, shape(half, jnp.bfloat16), 2)(got, held)
    far_got = lax.ppermute(send_got, "shard", swap)
    model = call(
        keep_kernel,
        shape((rows, kept_cols), jnp.float32),
        [VMEM] * 2 + [HBM],
        scratch=[pltpu.VMEM(near_shape.shape, jnp.bfloat16), pltpu.SemaphoreType.DMA((4,))],
    )(kept, got, basis)
    square = functools.partial(
        square_kernel, capacity=capacity, count=batches * experts * SEQS
    )
    total = shape((rank, kept_cols), jnp.float32)
    acc = call(functools.partial(square, side=0), total, 3)(model, far_kept, masked)
    out = call(functools.partial(square, side=1), total, 4)(model, far_got, masked, acc)
    return out[None, None]


def solution(mesh):
    return jax.shard_map(
        on_device,
        mesh=mesh,
        in_specs=(
            P("section", None, "expert", None),
            P("section", None, "expert", None),
            P(None, "expert", None),
            P(None, "expert", "shard"),
            P("section", None, "expert", "shard"),
            P("section", "expert", None, None, "shard"),
            P("section", "expert", "shard", None),
            P("section", "expert", "shard", None),
        ),
        out_specs=P("section", "expert", None, "shard"),
        check_vma=False,
    )
```

```python
import functools

import jax
import jax.numpy as jnp
from jax import lax
from jax.experimental import pallas as pl
from jax.experimental.pallas import tpu as pltpu
from jax.sharding import PartitionSpec as P

SEQS = 2
LANES = 128
COLS = 256


SECTIONS = 32


def ring(n):
    return n + n // 2 * (1 - n % 2 * 2)


def place_back(section):
    return SECTIONS - 1 - (ring(section // 2 % 4) * 8 + section % 2 * 4 + ring(section // 8))


def place_out(section):
    return place_back(section)


def scan_kernel(x_ref, top_ref, basis_ref, o_ref):
    count = x_ref.shape[0]
    state = top_ref[...].astype(jnp.float32)
    for section in range(count - 1, -1, -1):
        o_ref[place_back(section)] = state.astype(jnp.bfloat16)
        if section:
            state = state + x_ref[place_out(section)].astype(jnp.float32)


def prepare_kernel(
    routes_ref,
    probs_ref,
    ids_ref,
    top_ref,
    pick_ref,
    scale_ref,
    tag_ref,
    tag_sent_ref,
    start_ref,
    sems,
    *,
    capacity
):
    batches, _, tokens = routes_ref.shape
    mine = lax.axis_index("expert")
    place = place_out(lax.axis_index("section"))
    rows, part = start_ref.shape
    halves = top_ref.shape[1] // part
    loads = [
        pltpu.make_async_copy(
            top_ref.at[
                pl.ds(pl.multiple_of((place // halves) * rows, rows), rows),
                pl.ds(pl.multiple_of((place % halves) * part, part), part),
            ],
            start_ref,
            sems.at[0],
        ),
    ]
    for load in loads:
        load.start()
    before = (
        lax.broadcasted_iota(jnp.int32, (tokens, tokens), 0)
        < lax.broadcasted_iota(jnp.int32, (tokens, tokens), 1)
    ).astype(jnp.bfloat16)
    eye = lax.broadcasted_iota(jnp.int32, (tokens, tokens), 0) == lax.broadcasted_iota(
        jnp.int32, (tokens, tokens), 1
    )
    slot = lax.broadcasted_iota(jnp.int32, (capacity, tokens), 0).astype(jnp.float32)
    for m in range(batches):
        names = routes_ref[m]
        weights = probs_ref[m]
        examples = ids_ref[m : m + 1].astype(jnp.float32) + 1.0
        for side in range(2):
            hit2 = names == (1 - mine if side else mine)
            hit = jnp.sum(hit2.astype(jnp.float32), axis=0, keepdims=True)
            weight = jnp.sum(jnp.where(hit2, weights, 0.0), axis=0, keepdims=True)
            rank = jnp.dot(
                jnp.broadcast_to(hit, (8, tokens)).astype(jnp.bfloat16),
                before,
                preferred_element_type=jnp.float32,
            )[:1]
            chosen = (jnp.broadcast_to(rank, slot.shape) == slot) & (
                jnp.broadcast_to(hit, slot.shape) > 0.0
            )
            pick = chosen.astype(jnp.float32)
            blank = jnp.zeros(pick.shape, jnp.float32)
            row = jnp.concatenate([pick if n == m else blank for n in range(batches)], axis=1)
            pick_ref[side, pl.ds(m * capacity, capacity), :] = row.astype(jnp.bfloat16)
            tag = (
                jnp.sum(
                    jnp.where(chosen, jnp.broadcast_to(examples, slot.shape), 0.0),
                    axis=1,
                    keepdims=True,
                )
                - 1.0
            )
            (tag_sent_ref if side else tag_ref)[pl.ds(m * capacity, capacity), :] = (
                jnp.broadcast_to(tag, (capacity, LANES)).astype(jnp.bfloat16)
            )
            scale = jnp.sum(
                jnp.where(eye, jnp.broadcast_to(weight, eye.shape), 0.0),
                axis=1,
                keepdims=True,
            )
            scale_ref[side, pl.ds(m * tokens, tokens), :] = jnp.broadcast_to(
                scale, (tokens, LANES)
            )
    for load in loads:
        load.wait()


def hidden_kernel(acts_ref, basis_ref, out_ref, acts_held, basis_held, sems):
    count = sems.shape[1]
    depth = acts_ref.shape[1] // count
    copies = []
    for k in range(count):
        at = pl.ds(k * depth, depth)
        pair = (
            pltpu.make_async_copy(acts_ref.at[:, at], acts_held.at[:, at], sems.at[0, k]),
            pltpu.make_async_copy(basis_ref.at[at, :], basis_held.at[at, :], sems.at[1, k]),
        )
        for copy in pair:
            copy.start()
        copies.append(pair)
    total = None
    for k in range(count):
        at = pl.ds(k * depth, depth)
        for copy in copies[k]:
            copy.wait()
        part = jnp.dot(acts_held[:, at], basis_held[at, :], preferred_element_type=jnp.float32)
        total = part if total is None else total + part
    out_ref[...] = total


def mask_kernel(hidden_ref, far_ref, tag_ref, tag_far_ref, out_ref, *, capacity, owners):
    batches = hidden_ref.shape[0] // (owners * capacity)
    mine = lax.axis_index("expert")
    for side in range(2):
        owner = 1 - mine if side else mine
        for m in range(batches):
            slots = pl.ds(
                pl.multiple_of(m * owners * capacity + owner * capacity, capacity), capacity
            )
            at = pl.ds(m * capacity, capacity)
            hidden = hidden_ref[slots, :] + far_ref[slots, :].astype(jnp.float32)
            tag = (tag_far_ref if side else tag_ref)[at, :].astype(jnp.float32)
            tag = jnp.concatenate([tag] * (hidden.shape[1] // LANES), axis=1)
            for q in range(SEQS):
                out_ref[side, q, at, :] = jnp.where(tag == float(q), hidden, 0.0).astype(
                    jnp.bfloat16
                )


def where(piece):
    return next(place_back(n) for n in range(SECTIONS) if place_out(n) == piece)


def dispatch(later_ref, pick_ref, scale_ref, side, store):
    rows, part = later_ref.shape[1:]
    blocks = scale_ref.shape[1] // rows
    halves = later_ref.shape[0] // blocks
    step = 2 * LANES
    for h in range(halves):
        for c in range(0, part, step):
            values = []
            for b in range(blocks):
                value = later_ref[where(b * halves + h), :, pl.ds(c, step)].astype(jnp.float32)
                scale = scale_ref[side, pl.ds(b * rows, rows), :]
                values.append(value * jnp.concatenate([scale] * (step // LANES), axis=1))
            value = jnp.concatenate(values, axis=0).astype(jnp.bfloat16)
            store(
                h * part + c,
                step,
                jnp.dot(pick_ref[side], value, preferred_element_type=jnp.float32).astype(
                    jnp.bfloat16
                ),
            )


def sent_kernel(later_ref, pick_ref, scale_ref, basis_ref, out_ref):
    def store(at, size, value):
        out_ref[:, pl.ds(at, size)] = value

    dispatch(later_ref, pick_ref, scale_ref, 1, store)


def rotate(blocks, basis_ref, mine):
    half = basis_ref.shape[1] // 2
    place = lax.axis_index("shard")
    start = pl.multiple_of((place if mine else 1 - place) * half, half)
    rows = [ref[...] for ref in blocks]
    return jnp.dot(
        rows[0] if len(rows) == 1 else jnp.concatenate(rows, axis=0),
        basis_ref[:, pl.ds(start, half)],
        preferred_element_type=jnp.float32,
    )


def kept_kernel(later_ref, pick_ref, scale_ref, basis_ref, send_ref, rows_ref):
    def store(at, size, value):
        rows_ref[:, pl.ds(at, size)] = value

    dispatch(later_ref, pick_ref, scale_ref, 0, store)
    send_ref[...] = rotate([rows_ref], basis_ref, False).astype(send_ref.dtype)


def got_kernel(rows_ref, basis_ref, send_ref):
    send_ref[...] = rotate([rows_ref], basis_ref, False).astype(send_ref.dtype)


def keep_kernel(kept_ref, got_ref, basis_ref, out_ref):
    out_ref[...] = rotate([kept_ref, got_ref], basis_ref, True)


def squares(model_ref, far_ref, hidden_ref, side, cols, capacity, acc):
    rows = far_ref.shape[0]
    for m in range(rows // capacity):
        at = pl.ds(m * capacity, capacity)
        near = pl.ds(side * rows + m * capacity, capacity)
        model = (model_ref[near, cols] + far_ref[at, cols].astype(jnp.float32)).astype(
            jnp.bfloat16
        )
        for q in range(SEQS):
            grad = lax.dot_general(
                hidden_ref[side, q, at, :],
                model,
                (((0,), (0,)), ((), ())),
                preferred_element_type=jnp.float32,
            )
            acc = grad * grad if acc is None else acc + grad * grad
    return acc


def first_kernel(model_ref, far_ref, hidden_ref, out_ref, *, capacity):
    for c in range(0, out_ref.shape[1], COLS):
        cols = pl.ds(c, COLS)
        out_ref[:, cols] = squares(model_ref, far_ref, hidden_ref, 0, cols, capacity, None)


def last_kernel(
    model_ref, far_ref, hidden_ref, acc_ref, out_ref, done_ref, sems, *, capacity, count
):
    copies = []
    for k, c in enumerate(range(0, acc_ref.shape[1], COLS)):
        cols = pl.ds(c, COLS)
        total = squares(model_ref, far_ref, hidden_ref, 1, cols, capacity, acc_ref[:, cols])
        done_ref[:, cols] = total * (1.0 / count)
        copy = pltpu.make_async_copy(done_ref.at[:, cols], out_ref.at[:, cols], sems.at[k])
        copy.start()
        copies.append(copy)
    for copy in copies:
        copy.wait()


VMEM = pl.BlockSpec(memory_space=pltpu.VMEM)
HBM = pl.BlockSpec(memory_space=pltpu.HBM)


def call(body, shapes, ins, limit=8 << 20, scratch=(), cost=None, outs=None):
    single = not isinstance(shapes, (list, tuple))
    return pl.pallas_call(
        body,
        scratch_shapes=scratch,
        cost_estimate=cost,
        out_shape=shapes,
        in_specs=[VMEM] * ins if isinstance(ins, int) else ins,
        out_specs=outs or (VMEM if single else [VMEM] * len(shapes)),
        compiler_params=pltpu.CompilerParams(vmem_limit_bytes=limit),
    )


def on_device(
    routes,
    route_probs,
    example_ids,
    top_cotangent,
    branch_cotangent,
    hidden_acts,
    basis_hidden,
    basis_model,
):
    experts = lax.axis_size("expert")
    shards = lax.axis_size("shard")
    sections = lax.axis_size("section")
    batches, tokens, width = top_cotangent.shape
    slots = hidden_acts.shape[3]
    capacity = slots // experts
    cols = basis_model.shape[3]
    kept_cols = cols // shards
    rank = basis_hidden.shape[3]
    rows = batches * experts * capacity
    block = 8
    groups = batches * tokens // block
    halves = sections // groups
    part = width // halves

    swap = [(0, 1), (1, 0)]
    shape = jax.ShapeDtypeStruct
    fixed = functools.partial(pltpu.with_memory_space_constraint, memory_space=pltpu.HBM)
    basis = basis_model[0, 0]
    acts = hidden_acts[0, 0].reshape(rows, -1)
    hidden = call(
        hidden_kernel,
        shape((rows, rank), jnp.float32),
        [HBM] * 2,
        limit=16 << 20,
        scratch=[
            pltpu.VMEM(acts.shape, jnp.bfloat16),
            pltpu.VMEM(basis_hidden.shape[2:], jnp.bfloat16),
            pltpu.SemaphoreType.DMA((2, 8)),
        ],
    )(fixed(acts), fixed(basis_hidden[0, 0]))
    pieces = (
        branch_cotangent[0]
        .reshape(groups, block, halves, part)
        .transpose(0, 2, 1, 3)
        .reshape(sections, block, part)
    )
    hidden_far = lax.ppermute(hidden.astype(jnp.bfloat16), "shard", swap)
    tag_shape = shape((batches * capacity, LANES), jnp.bfloat16)
    prepare = call(
        functools.partial(prepare_kernel, capacity=capacity),
        [
            shape((2, batches * capacity, batches * tokens), jnp.bfloat16),
            shape((2, batches * tokens, LANES), jnp.float32),
            tag_shape,
            tag_shape,
            shape((block, part), jnp.bfloat16),
        ],
        [VMEM] * 3 + [HBM],
        scratch=[pltpu.SemaphoreType.DMA((1,))],
    )
    pick, scale, tag, tag_sent, start = prepare(
        routes[0].transpose(0, 2, 1),
        route_probs[0].transpose(0, 2, 1),
        example_ids[:, 0],
        fixed(top_cotangent.reshape(batches * tokens, width)),
    )
    tag_far = lax.ppermute(tag_sent, "expert", swap)
    out_order = [sorted(range(sections), key=place_out)]
    back_order = [sorted(range(sections), key=place_back)]
    layers = lax.all_to_all(
        pieces, "section", 0, 0, tiled=True, axis_index_groups=out_order
    )
    layers = call(scan_kernel, shape(layers.shape, jnp.bfloat16), [VMEM, VMEM, HBM])(layers, start, fixed(basis))
    layers, hidden, pick, scale, tag = lax.optimization_barrier(
        (layers, hidden, pick, scale, tag)
    )
    later = lax.all_to_all(layers, "section", 0, 0, tiled=True, axis_index_groups=back_order)
    masked = call(
        functools.partial(mask_kernel, capacity=capacity, owners=experts),
        shape((2, SEQS, batches * capacity, rank), jnp.bfloat16),
        4,
    )(hidden, hidden_far, tag, tag_far)
    half = (batches * capacity, kept_cols)
    row_shape = shape((batches * capacity, width), jnp.bfloat16)
    sent = call(sent_kernel, row_shape, [VMEM] * 3 + [HBM])(later, pick, scale, fixed(basis))
    got = lax.ppermute(sent, "expert", swap)
    send_kept, kept = call(kept_kernel, [shape(half, jnp.bfloat16), row_shape], 4)(
        later, pick, scale, basis
    )
    far_kept = lax.ppermute(send_kept, "shard", swap)
    send_got = call(got_kernel, shape(half, jnp.bfloat16), 2)(got, basis)
    far_got = lax.ppermute(send_got, "shard", swap)
    model = call(keep_kernel, shape((rows, kept_cols), jnp.float32), 3)(kept, got, basis)
    total = shape((rank, kept_cols), jnp.float32)
    acc = call(functools.partial(first_kernel, capacity=capacity), total, 3)(
        model, far_kept, masked
    )
    out = call(
        functools.partial(
            last_kernel, capacity=capacity, count=batches * experts * SEQS
        ),
        total,
        4,
        scratch=[
            pltpu.VMEM(total.shape, jnp.float32),
            pltpu.SemaphoreType.DMA((kept_cols // COLS,)),
        ],
        outs=HBM,
    )(model, far_got, masked, acc)
    return out[None, None]


def solution(mesh):
    return jax.shard_map(
        on_device,
        mesh=mesh,
        in_specs=(
            P("section", None, "expert", None),
            P("section", None, "expert", None),
            P(None, "expert", None),
            P(None, "expert", "shard"),
            P("section", None, "expert", "shard"),
            P("section", "expert", None, None, "shard"),
            P("section", "expert", "shard", None),
            P("section", "expert", "shard", None),
        ),
        out_specs=P("section", "expert", None, "shard"),
        check_vma=False,
    )
```

```python
import functools

import jax
import jax.numpy as jnp
from jax import lax
from jax.experimental import pallas as pl
from jax.experimental.pallas import tpu as pltpu
from jax.sharding import PartitionSpec as P

SEQS = 2
LANES = 128
ROWS = 128


SECTIONS = 32


def ring(n):
    return n + n // 2 * (1 - n % 2 * 2)


def place_back(section):
    return SECTIONS - 1 - (ring(section // 2 % 4) * 8 + section % 2 * 4 + ring(section // 8))


def place_out(section):
    return place_back(section)


def scan_kernel(x_ref, top_ref, basis_ref, o_ref):
    count = x_ref.shape[0]
    state = top_ref[...].astype(jnp.float32)
    for section in range(count - 1, -1, -1):
        o_ref[place_back(section)] = state.astype(jnp.bfloat16)
        if section:
            state = state + x_ref[place_out(section)].astype(jnp.float32)


def prepare_kernel(
    routes_ref,
    probs_ref,
    ids_ref,
    top_ref,
    pick_ref,
    scale_ref,
    tag_ref,
    tag_sent_ref,
    start_ref,
    sems,
    *,
    capacity
):
    batches, _, tokens = routes_ref.shape
    mine = lax.axis_index("expert")
    place = place_out(lax.axis_index("section"))
    rows, part = start_ref.shape
    halves = top_ref.shape[1] // part
    loads = [
        pltpu.make_async_copy(
            top_ref.at[
                pl.ds(pl.multiple_of((place // halves) * rows, rows), rows),
                pl.ds(pl.multiple_of((place % halves) * part, part), part),
            ],
            start_ref,
            sems.at[0],
        ),
    ]
    for load in loads:
        load.start()
    before = (
        lax.broadcasted_iota(jnp.int32, (tokens, tokens), 0)
        < lax.broadcasted_iota(jnp.int32, (tokens, tokens), 1)
    ).astype(jnp.bfloat16)
    eye = lax.broadcasted_iota(jnp.int32, (tokens, tokens), 0) == lax.broadcasted_iota(
        jnp.int32, (tokens, tokens), 1
    )
    slot = lax.broadcasted_iota(jnp.int32, (capacity, tokens), 0).astype(jnp.float32)
    for m in range(batches):
        names = routes_ref[m]
        weights = probs_ref[m]
        examples = ids_ref[m : m + 1].astype(jnp.float32) + 1.0
        for side in range(2):
            hit2 = names == (1 - mine if side else mine)
            hit = jnp.sum(hit2.astype(jnp.float32), axis=0, keepdims=True)
            weight = jnp.sum(jnp.where(hit2, weights, 0.0), axis=0, keepdims=True)
            rank = jnp.dot(
                jnp.broadcast_to(hit, (8, tokens)).astype(jnp.bfloat16),
                before,
                preferred_element_type=jnp.float32,
            )[:1]
            chosen = (jnp.broadcast_to(rank, slot.shape) == slot) & (
                jnp.broadcast_to(hit, slot.shape) > 0.0
            )
            pick = chosen.astype(jnp.float32)
            blank = jnp.zeros(pick.shape, jnp.float32)
            row = jnp.concatenate([pick if n == m else blank for n in range(batches)], axis=1)
            pick_ref[side, pl.ds(m * capacity, capacity), :] = row.astype(jnp.bfloat16)
            tag = (
                jnp.sum(
                    jnp.where(chosen, jnp.broadcast_to(examples, slot.shape), 0.0),
                    axis=1,
                    keepdims=True,
                )
                - 1.0
            )
            (tag_sent_ref if side else tag_ref)[pl.ds(m * capacity, capacity), :] = (
                jnp.broadcast_to(tag, (capacity, LANES)).astype(jnp.bfloat16)
            )
            scale = jnp.sum(
                jnp.where(eye, jnp.broadcast_to(weight, eye.shape), 0.0),
                axis=1,
                keepdims=True,
            )
            scale_ref[side, pl.ds(m * tokens, tokens), :] = jnp.broadcast_to(
                scale, (tokens, LANES)
            )
    for load in loads:
        load.wait()


def hidden_kernel(acts_ref, basis_ref, out_ref, acts_held, basis_held, sems):
    count = sems.shape[1]
    depth = acts_ref.shape[1] // count
    copies = []
    for k in range(count):
        at = pl.ds(k * depth, depth)
        pair = (
            pltpu.make_async_copy(acts_ref.at[:, at], acts_held.at[:, at], sems.at[0, k]),
            pltpu.make_async_copy(basis_ref.at[at, :], basis_held.at[at, :], sems.at[1, k]),
        )
        for copy in pair:
            copy.start()
        copies.append(pair)
    total = None
    for k in range(count):
        at = pl.ds(k * depth, depth)
        for copy in copies[k]:
            copy.wait()
        part = jnp.dot(acts_held[:, at], basis_held[at, :], preferred_element_type=jnp.float32)
        total = part if total is None else total + part
    out_ref[...] = total


def pair_weight(shift, capacity):
    return 1.0 if shift in (0, capacity // 2) else 2.0


def hidden_pairs_kernel(
    hidden_ref, far_ref, tag_ref, tag_far_ref, out_ref, *, capacity, owners
):
    batches = hidden_ref.shape[0] // (owners * capacity)
    mine = lax.axis_index("expert")
    pairs = []
    for side in range(2):
        owner = 1 - mine if side else mine
        for m in range(batches):
            slots = pl.ds(
                pl.multiple_of(m * owners * capacity + owner * capacity, capacity), capacity
            )
            hidden = hidden_ref[slots, :] + far_ref[slots, :].astype(jnp.float32)
            hidden = hidden.astype(jnp.bfloat16).astype(jnp.float32)
            tag = (tag_far_ref if side else tag_ref)[pl.ds(m * capacity, capacity), :]
            tag = tag.astype(jnp.float32)
            for shift in range(capacity // 2 + 1):
                other = pltpu.roll(hidden, shift, 0) if shift else hidden
                other_tag = pltpu.roll(tag, shift, 0) if shift else tag
                weight = jnp.where(
                    (tag == other_tag) & (tag >= 0.0), pair_weight(shift, capacity), 0.0
                )
                weight = jnp.concatenate([weight] * (hidden.shape[1] // LANES), axis=1)
                pairs.append(hidden * other * weight)
    out_ref[...] = jnp.concatenate(pairs, axis=0).T.astype(jnp.bfloat16)


def where(piece):
    return next(place_back(n) for n in range(SECTIONS) if place_out(n) == piece)


def dispatch(later_ref, pick_ref, scale_ref, side, store):
    rows, part = later_ref.shape[1:]
    blocks = scale_ref.shape[1] // rows
    halves = later_ref.shape[0] // blocks
    step = 2 * LANES
    for h in range(halves):
        for c in range(0, part, step):
            values = []
            for b in range(blocks):
                value = later_ref[where(b * halves + h), :, pl.ds(c, step)].astype(jnp.float32)
                scale = scale_ref[side, pl.ds(b * rows, rows), :]
                values.append(value * jnp.concatenate([scale] * (step // LANES), axis=1))
            value = jnp.concatenate(values, axis=0).astype(jnp.bfloat16)
            store(
                h * part + c,
                step,
                jnp.dot(pick_ref[side], value, preferred_element_type=jnp.float32).astype(
                    jnp.bfloat16
                ),
            )


def sent_kernel(later_ref, pick_ref, scale_ref, basis_ref, out_ref):
    def store(at, size, value):
        out_ref[:, pl.ds(at, size)] = value

    dispatch(later_ref, pick_ref, scale_ref, 1, store)


def rotate(blocks, basis_ref, mine):
    half = basis_ref.shape[1] // 2
    place = lax.axis_index("shard")
    start = pl.multiple_of((place if mine else 1 - place) * half, half)
    rows = [ref[...] for ref in blocks]
    return jnp.dot(
        rows[0] if len(rows) == 1 else jnp.concatenate(rows, axis=0),
        basis_ref[:, pl.ds(start, half)],
        preferred_element_type=jnp.float32,
    )


def kept_kernel(later_ref, pick_ref, scale_ref, out_ref):
    def store(at, size, value):
        out_ref[:, pl.ds(at, size)] = value

    dispatch(later_ref, pick_ref, scale_ref, 0, store)


def both_kernel(kept_ref, got_ref, basis_ref, out_ref):
    out_ref[...] = rotate([kept_ref, got_ref], basis_ref, False).astype(out_ref.dtype)


def keep_kernel(kept_ref, got_ref, basis_ref, out_ref):
    out_ref[...] = rotate([kept_ref, got_ref], basis_ref, True)


def last_kernel(
    model_ref, far_ref, pairs_ref, out_ref, model_pairs_ref, done_ref, sems, *, capacity, count
):
    shifts = capacity // 2 + 1
    for m in range(model_ref.shape[0] // capacity):
        at = pl.ds(m * capacity, capacity)
        model = (model_ref[at, :] + far_ref[at, :].astype(jnp.float32)).astype(jnp.bfloat16)
        model = model.astype(jnp.float32)
        for shift in range(shifts):
            other = pltpu.roll(model, shift, 0) if shift else model
            model_pairs_ref[pl.ds((m * shifts + shift) * capacity, capacity), :] = (
                model * other
            ).astype(jnp.bfloat16)
    copies = []
    for k in range(sems.shape[0]):
        at = pl.ds(k * ROWS, ROWS)
        total = jnp.dot(
            pairs_ref[at, :], model_pairs_ref[...], preferred_element_type=jnp.float32
        )
        done_ref[at, :] = total * (1.0 / count)
        copy = pltpu.make_async_copy(done_ref.at[at, :], out_ref.at[at, :], sems.at[k])
        copy.start()
        copies.append(copy)
    for copy in copies:
        copy.wait()


VMEM = pl.BlockSpec(memory_space=pltpu.VMEM)
HBM = pl.BlockSpec(memory_space=pltpu.HBM)


def call(body, shapes, ins, limit=8 << 20, scratch=(), cost=None, outs=None):
    single = not isinstance(shapes, (list, tuple))
    return pl.pallas_call(
        body,
        scratch_shapes=scratch,
        cost_estimate=cost,
        out_shape=shapes,
        in_specs=[VMEM] * ins if isinstance(ins, int) else ins,
        out_specs=outs or (VMEM if single else [VMEM] * len(shapes)),
        compiler_params=pltpu.CompilerParams(vmem_limit_bytes=limit),
    )


def on_device(
    routes,
    route_probs,
    example_ids,
    top_cotangent,
    branch_cotangent,
    hidden_acts,
    basis_hidden,
    basis_model,
):
    experts = lax.axis_size("expert")
    shards = lax.axis_size("shard")
    sections = lax.axis_size("section")
    batches, tokens, width = top_cotangent.shape
    slots = hidden_acts.shape[3]
    capacity = slots // experts
    cols = basis_model.shape[3]
    kept_cols = cols // shards
    rank = basis_hidden.shape[3]
    rows = batches * experts * capacity
    block = 8
    groups = batches * tokens // block
    halves = sections // groups
    part = width // halves

    swap = [(0, 1), (1, 0)]
    shape = jax.ShapeDtypeStruct
    fixed = functools.partial(pltpu.with_memory_space_constraint, memory_space=pltpu.HBM)
    basis = basis_model[0, 0]
    acts = hidden_acts[0, 0].reshape(rows, -1)
    hidden = call(
        hidden_kernel,
        shape((rows, rank), jnp.float32),
        [HBM] * 2,
        limit=16 << 20,
        scratch=[
            pltpu.VMEM(acts.shape, jnp.bfloat16),
            pltpu.VMEM(basis_hidden.shape[2:], jnp.bfloat16),
            pltpu.SemaphoreType.DMA((2, 8)),
        ],
    )(fixed(acts), fixed(basis_hidden[0, 0]))
    pieces = (
        branch_cotangent[0]
        .reshape(groups, block, halves, part)
        .transpose(0, 2, 1, 3)
        .reshape(sections, block, part)
    )
    hidden_far = lax.ppermute(hidden, "shard", swap)
    tag_shape = shape((batches * capacity, LANES), jnp.bfloat16)
    prepare = call(
        functools.partial(prepare_kernel, capacity=capacity),
        [
            shape((2, batches * capacity, batches * tokens), jnp.bfloat16),
            shape((2, batches * tokens, LANES), jnp.float32),
            tag_shape,
            tag_shape,
            shape((block, part), jnp.bfloat16),
        ],
        [VMEM] * 3 + [HBM],
        scratch=[pltpu.SemaphoreType.DMA((1,))],
    )
    pick, scale, tag, tag_sent, start = prepare(
        routes[0].transpose(0, 2, 1),
        route_probs[0].transpose(0, 2, 1),
        example_ids[:, 0],
        fixed(top_cotangent.reshape(batches * tokens, width)),
    )
    tag_far = lax.ppermute(tag_sent, "expert", swap)
    out_order = [sorted(range(sections), key=place_out)]
    back_order = [sorted(range(sections), key=place_back)]
    layers = lax.all_to_all(
        pieces, "section", 0, 0, tiled=True, axis_index_groups=out_order
    )
    layers = call(scan_kernel, shape(layers.shape, jnp.bfloat16), [VMEM, VMEM, HBM])(layers, start, fixed(basis))
    layers, hidden, pick, scale, tag = lax.optimization_barrier(
        (layers, hidden, pick, scale, tag)
    )
    later = lax.all_to_all(layers, "section", 0, 0, tiled=True, axis_index_groups=back_order)
    pair_rows = rows * (capacity // 2 + 1)
    pairs = call(
        functools.partial(hidden_pairs_kernel, capacity=capacity, owners=experts),
        shape((rank, pair_rows), jnp.bfloat16),
        4,
    )(hidden, hidden_far, tag, tag_far)
    row_shape = shape((batches * capacity, width), jnp.bfloat16)
    sent = call(sent_kernel, row_shape, [VMEM] * 3 + [HBM])(later, pick, scale, fixed(basis))
    got = lax.ppermute(sent, "expert", swap)
    kept = call(kept_kernel, row_shape, 3)(later, pick, scale)
    send = call(both_kernel, shape((rows, kept_cols), jnp.bfloat16), 3)(kept, got, basis)
    far = lax.ppermute(send, "shard", swap)
    model = call(keep_kernel, shape((rows, kept_cols), jnp.float32), 3)(kept, got, basis)
    total = shape((rank, kept_cols), jnp.float32)
    out = call(
        functools.partial(
            last_kernel, capacity=capacity, count=batches * experts * SEQS
        ),
        total,
        3,
        scratch=[
            pltpu.VMEM((pair_rows, kept_cols), jnp.bfloat16),
            pltpu.VMEM(total.shape, jnp.float32),
            pltpu.SemaphoreType.DMA((rank // ROWS,)),
        ],
        outs=HBM,
    )(model, far, pairs)
    return out[None, None]


def solution(mesh):
    return jax.shard_map(
        on_device,
        mesh=mesh,
        in_specs=(
            P("section", None, "expert", None),
            P("section", None, "expert", None),
            P(None, "expert", None),
            P(None, "expert", "shard"),
            P("section", None, "expert", "shard"),
            P("section", "expert", None, None, "shard"),
            P("section", "expert", "shard", None),
            P("section", "expert", "shard", None),
        ),
        out_specs=P("section", "expert", None, "shard"),
        check_vma=False,
    )
```
